256 devices in a mesh: op: 4 (over x), sec: 64 (over z, y, core).
Axes of the slice: x: 4, y: 4, z: 8, core: 2. Of those that a mesh axis runs over, the one named last changes fastest.
Arguments:
- wavefunction: bfloat16 [4096, 128, 128], P('sec'), may hold values from -6 to 6
- left_ops: bfloat16 [2, 16, 8, 128, 128], P(None, 'op'), may hold values from -0.5 to 0.5
- right_ops: bfloat16 [2, 16, 8, 128, 128], P(None, 'op'), may hold values from -0.09375 to 0.09375
- left_sector: int32 [4096], P('sec'), may hold values from 0 to 7
- right_sector: int32 [4096], P('sec'), may hold values from 0 to 7
- target: int32 [2, 4096], replicated, may hold values from 0 to 4095, as said below
Outputs:
- applied_blocks: float32 [4096, 128, 128], P('sec', 'op')
The draws below stay inside these ranges and needn't reach their ends.
Inputs may be any that keep to these rules, and one draw needn't show every extreme that they name: For every class, target is a permutation of the 4096 blocks; block b lies on index b // 64 of sec, and for every class exactly 1 of the blocks of one index of sec map to blocks of each index of sec.
All inputs are finite; a program needn't handle non-finite values.
Results may differ from the reference program's by a relative error of at most 0.0029.
Values may be sent and summed in bfloat16 or wider, within the bound.
No kernel may reach another device: no remote copies, remote signals or barrier semaphores. Data moves between devices by JAX's collectives and lax.ppermute only.
A program may use at most 64 MiB of HBM per device.

```python
import jax
import jax.numpy as jnp
from jax import lax

BL = 128
BR = 128
NL = 8
NR = 8
CLASSES = 2
BLOCK_DEV = 64
TERMS = 16
BLOCKS = 4096


def draw_target(key, part):
    shards = BLOCKS // BLOCK_DEV
    rows_out = []
    for class_index in range(CLASSES):
        keys = jax.random.split(jax.random.fold_in(key, 7001 + class_index), 3)
        device_perm = jax.random.permutation(keys[0], shards)
        offset_perm = jax.random.permutation(keys[1], shards)
        slot_perm = jax.random.permutation(keys[2], BLOCK_DEV)
        device_ids = jnp.arange(shards, dtype=jnp.int32)[:, None]
        slot_ids = jnp.arange(BLOCK_DEV, dtype=jnp.int32)[None, :]
        dest_device = (device_perm[device_ids] + offset_perm[slot_ids % shards]) % shards
        mapped = dest_device * BLOCK_DEV + slot_perm[slot_ids]
        rows_out.append(mapped.reshape(-1))
    return jnp.stack(rows_out).astype(jnp.int32)


def plant(array, stream_key, low, high):
    extent = array.shape
    index_at = [jax.random.randint(jax.random.fold_in(stream_key, axis), (), 0, extent[axis]) for axis in range(len(extent))]
    array = array.at[tuple(index_at)].set(low)
    longest = extent.index(max(extent))
    index_at[longest] = (index_at[longest] + 1) % extent[longest]
    return array.at[tuple(index_at)].set(high)


def level_of(stream_key, extent, pieces, smallest, top_value):
    factor_of, own = 1.0, jax.random.fold_in(stream_key, 6)
    for axis_at, parts in pieces:
        steps = jnp.exp(jax.random.uniform(jax.random.fold_in(own, axis_at), (parts,), jnp.float32, smallest / len(pieces), top_value / len(pieces)))
        factor_of = factor_of * jnp.repeat(steps, extent[axis_at] // parts).reshape([-1 if axis == axis_at else 1 for axis in range(len(extent))])
    return factor_of


def scatter_about(stream_key, shape, scale, bound, cuts=(), held_as=jnp.bfloat16):
    entries = scale * jax.random.normal(stream_key, shape, jnp.float32)
    if cuts:
        entries = entries * level_of(stream_key, shape, cuts, -0.22, 0.18)
    return jnp.clip(entries, -bound, bound).astype(held_as)


def setup_inputs(seed: int = 0) -> dict:
    key_of = jax.random.split(jax.random.key(seed), 7)
    wavefunction = scatter_about(key_of[0], (BLOCKS, BL, BR), 1.0, 6.0, ((0, 64),))
    left_ops = scatter_about(key_of[1], (CLASSES, TERMS, NL, BL, BL), BL ** -0.5, 0.5, ((1, 4),))
    right_ops = scatter_about(key_of[2], (CLASSES, TERMS, NR, BR, BR), (BR * CLASSES * TERMS) ** -0.5, 0.09375, ((1, 4),))
    left_sector = plant(jax.random.randint(key_of[3], (BLOCKS,), 0, NL), jax.random.fold_in(key_of[3], 1), 0, NL - 1).astype(jnp.int32)
    right_sector = plant(jax.random.randint(key_of[4], (BLOCKS,), 0, NR), jax.random.fold_in(key_of[4], 1), 0, NR - 1).astype(jnp.int32)
    target = draw_target(jax.random.fold_in(key_of[6], 71), 0)
    return {"wavefunction": wavefunction, "left_ops": left_ops, "right_ops": right_ops, "left_sector": left_sector, "right_sector": right_sector, "target": target}


def reference(wavefunction, left_ops, right_ops, left_sector, right_sector, target):
    wave_float = wavefunction.astype(jnp.float32)
    applied = jnp.zeros(wavefunction.shape, jnp.float32)
    for class_index in range(CLASSES):
        def term_step(running, operators):
            left_term, right_term = operators
            left_blocks = jnp.take(left_term, left_sector, axis=0).astype(jnp.float32)
            right_blocks = jnp.take(right_term, right_sector, axis=0).astype(jnp.float32)
            mixed = jnp.einsum("bij,bjk->bik", left_blocks, wave_float).astype(jnp.bfloat16)
            mixed = lax.optimization_barrier(mixed).astype(jnp.float32)
            return running + jnp.einsum("bik,blk->bil", mixed, right_blocks), None

        initial = jnp.zeros(wavefunction.shape, jnp.float32)
        running, _ = lax.scan(term_step, initial, (left_ops[class_index], right_ops[class_index]))
        applied = applied.at[target[class_index]].add(running)
    return applied
```

```python
import functools

import jax
import jax.numpy as jnp
from jax import lax
from jax.experimental import pallas as pl
from jax.experimental.pallas import tpu as pltpu
from jax.sharding import PartitionSpec as P

F32, BF16 = jnp.float32, jnp.bfloat16


def apply_kernel(op_ref, target_ref, lsec_ref, rsec_ref, wave_ref, left_ref, right_ref, *outs, chunk, shards_of, per):
    terms, rows = left_ref.shape[1], left_ref.shape[3]
    op_size = rows // per
    half = per // 2
    own_op = op_ref[0]
    base = pl.program_id(0) * chunk
    offsets = [pl.multiple_of(lax.rem(own_op + r, op_size) * per, per) for r in range(op_size)]

    def one(i):
        b = base + i
        ls, rs = lsec_ref[b], rsec_ref[b]
        place = target_ref[b] // shards_of
        w = wave_ref[i]
        stacked = jnp.concatenate(
            [left_ref[0, t, ls, pl.ds(off, per), :] for t in range(terms) for off in offsets], axis=0
        )
        mixed = jnp.dot(stacked, w, preferred_element_type=F32).astype(BF16)
        lhs = jnp.concatenate([mixed[t * rows : (t + 1) * rows] for t in range(terms)], axis=1)
        rhs = jnp.concatenate([right_ref[0, t, rs] for t in range(terms)], axis=1)
        acc = lax.dot_general(lhs, rhs, (((1,), (1,)), ((), ())), preferred_element_type=F32)
        outs[0][place] = acc[:per]
        for k, out in enumerate(outs[1:]):
            lo = per + k * half
            out[place] = acc[lo : lo + half].astype(BF16)

    def body(i, carry):
        one(i)
        return carry

    lax.fori_loop(0, chunk, body, 0, unroll=2)


def apply_class(q, own_op, own_target, left_sector, right_sector, wavefunction, left_ops, right_ops):
    blocks, rows, cols = wavefunction.shape
    _, terms, sectors, _, _ = left_ops.shape
    op_size = lax.axis_size("op")
    per = rows // op_size
    chunk = 16
    ops_block = (1, terms, sectors, rows, rows)
    rops_block = (1, terms, right_ops.shape[2], cols, cols)
    outs = [jax.ShapeDtypeStruct((blocks, per, cols), F32)] + [
        jax.ShapeDtypeStruct((blocks, per // 2, cols), BF16) for _ in range(2 * (op_size - 1))
    ]
    flops = 2 * blocks * terms * (rows * rows * cols + rows * cols * cols)
    return pl.pallas_call(
        functools.partial(apply_kernel, chunk=chunk, shards_of=blocks, per=per),
        out_shape=outs,
        grid_spec=pltpu.PrefetchScalarGridSpec(
            num_scalar_prefetch=4,
            grid=(blocks // chunk,),
            in_specs=[
                pl.BlockSpec((chunk, rows, cols), lambda g, *_: (g, 0, 0)),
                pl.BlockSpec(ops_block, lambda g, *_: (q, 0, 0, 0, 0)),
                pl.BlockSpec(rops_block, lambda g, *_: (q, 0, 0, 0, 0)),
            ],
            out_specs=[pl.BlockSpec(o.shape, lambda g, *_: (0, 0, 0)) for o in outs],
        ),
        cost_estimate=pl.CostEstimate(flops=flops, bytes_accessed=8 << 20, transcendentals=0),
        name=f"apply_class_{q}",
    )(own_op, own_target[q], left_sector, right_sector, wavefunction, left_ops, right_ops)


def place_kernel(slot_ref, arrived_ref, out_ref):
    sources, classes = arrived_ref.shape[:2]
    for q in range(classes):

        def body(s, carry):
            slot = slot_ref[q, s]
            block = arrived_ref[s, q].astype(F32)
            out_ref[slot] = block if q == 0 else out_ref[slot] + block
            return carry

        lax.fori_loop(0, sources, body, 0, unroll=4)


def op_exchange(parts, up, down):
    own, o1a, o1b, o2a, o2b, o3a, o3b = parts
    half = o1a.shape[1]
    ra, rb = up(o2a), down(o2b)
    q1, q3 = up(o1b), down(o3a)
    ca = up((o1a.astype(F32) + ra.astype(F32)).astype(BF16))
    cb = down((o3b.astype(F32) + rb.astype(F32)).astype(BF16))
    top = own[:, :half] + q3.astype(F32) + ca.astype(F32)
    bottom = own[:, half:] + q1.astype(F32) + cb.astype(F32)
    return jnp.concatenate([top, bottom], axis=1).astype(BF16)


def per_device(wavefunction, left_ops, right_ops, left_sector, right_sector, target):
    shards = lax.axis_size("sec")
    op_size = lax.axis_size("op")
    own_sec, own_op = lax.axis_index("sec"), lax.axis_index("op")
    blocks, rows, cols = wavefunction.shape
    classes = target.shape[0]
    own_target = lax.dynamic_slice(target, (0, own_sec * blocks), (classes, blocks))
    op_scalar = own_op.astype(jnp.int32).reshape(1)
    by_source = target.reshape(classes, shards, blocks)
    slots = jnp.sum(jnp.where(by_source // blocks == own_sec, by_source % blocks, 0), axis=2)
    up = functools.partial(lax.ppermute, axis_name="op", perm=[(i, (i + 1) % op_size) for i in range(op_size)])
    down = functools.partial(lax.ppermute, axis_name="op", perm=[(i, (i - 1) % op_size) for i in range(op_size)])
    sums = []
    for q in range(classes):
        parts = apply_class(q, op_scalar, own_target, left_sector, right_sector, wavefunction, left_ops, right_ops)
        sums.append(op_exchange(parts, up, down))
    arrived = lax.all_to_all(jnp.stack(sums, axis=1), "sec", split_axis=0, concat_axis=0, tiled=True)
    per = rows // op_size
    return pl.pallas_call(
        place_kernel,
        out_shape=jax.ShapeDtypeStruct((blocks, per, cols), F32),
        grid_spec=pltpu.PrefetchScalarGridSpec(
            num_scalar_prefetch=1,
            grid=(1,),
            in_specs=[pl.BlockSpec(arrived.shape, lambda g, *_: (0, 0, 0, 0))],
            out_specs=pl.BlockSpec((blocks, per, cols), lambda g, *_: (0, 0, 0)),
        ),
        name="place_blocks",
    )(slots, arrived)


def solution(mesh):
    in_specs = (
        P("sec", None, None),
        P(None, "op", None, None, None),
        P(None, "op", None, None, None),
        P("sec"),
        P("sec"),
        P(),
    )
    return jax.shard_map(
        per_device, mesh=mesh, in_specs=in_specs, out_specs=P("sec", "op", None), check_vma=False
    )
```

```python
import functools

import jax
import jax.numpy as jnp
from jax import lax
from jax.experimental import pallas as pl
from jax.experimental.pallas import tpu as pltpu
from jax.sharding import PartitionSpec as P


F32, BF16 = jnp.float32, jnp.bfloat16
GROUP = 32
PARTS = (((0, 16), (16, 16)), ((0, 32),))
JOINED = (((0, 0),), ((0, 1),), ((1, 0),))
BATCHES = (((0, 0), (0, 1)), ((1, 0),))
MIB = 1 << 20


def apply_kernel(target_hbm, lsec_hbm, rsec_hbm, wave_hbm, left_hbm, right_hbm, *refs, q, per):
    outs, (wave, left, right, mixed_ref, target, lsec, rsec, small_sem, left_sem, right_sem, wave_sem) = refs[:-11], refs[-11:]
    blocks, rows, cols = wave.shape
    terms = left.shape[0]
    op_size = rows // per
    own_op, own_sec = lax.axis_index("op"), lax.axis_index("sec")
    width = target.shape[1]
    window = pl.multiple_of(own_sec * blocks // width * width, width)
    first = lax.rem(own_sec * blocks, width)
    small = [
        pltpu.make_async_copy(target_hbm.at[:, pl.ds(window, width)], target, small_sem.at[0]),
        pltpu.make_async_copy(lsec_hbm, lsec, small_sem.at[1]),
        pltpu.make_async_copy(rsec_hbm, rsec, small_sem.at[2]),
    ]
    lefts = [pltpu.make_async_copy(left_hbm.at[q, t], left.at[t], left_sem.at[t]) for t in range(terms)]
    rights = [pltpu.make_async_copy(right_hbm.at[q, t], right.at[t], right_sem.at[t]) for t in range(terms)]

    def wave_copy(g):
        part = pl.ds(g * GROUP, GROUP)
        return pltpu.make_async_copy(wave_hbm.at[part], wave.at[part], wave_sem.at[g])

    for copy in small + lefts:
        copy.start()
    wave_copy(0).start()
    for copy in rights:
        copy.start()
    for g in range(1, blocks // GROUP):
        wave_copy(g).start()
    offsets = [pl.multiple_of(lax.rem(own_op + r, op_size) * per, per) for r in range(op_size)]
    for copy in small + lefts:
        copy.wait()

    def step(g, carry):
        wave_copy(g).wait()
        for i in range(GROUP):
            b = g * GROUP + i
            ls = lsec[b]
            stacked = jnp.concatenate([left[t, ls, pl.ds(off, per), :] for t in range(terms) for off in offsets], axis=0)
            mixed = jnp.dot(stacked, wave[b], preferred_element_type=F32).astype(BF16)
            for t in range(terms):
                mixed_ref[i, :, t * cols : (t + 1) * cols] = mixed[t * rows : (t + 1) * rows]

        @pl.when(g == 0)
        def _():
            for copy in rights:
                copy.wait()

        for i in range(GROUP):
            b = g * GROUP + i
            rs = rsec[b]
            place = target[q, first + b] // blocks
            rhs = jnp.concatenate([right[t, rs] for t in range(terms)], axis=1)
            acc = lax.dot_general(mixed_ref[i], rhs, (((1,), (1,)), ((), ())), preferred_element_type=F32)
            low = place < blocks // 2
            for k, (start, count) in enumerate(PARTS[q]):
                own, first_up, first_down, second = outs[4 * k : 4 * k + 4]
                zero, one, two, three = (acc[r * per + start : r * per + start + count] for r in range(op_size))
                one, two, three = (v.astype(BF16) for v in (one, two, three))
                own[place] = zero
                first_up[place] = jnp.where(low, two, one)
                first_down[place] = jnp.where(low, three, two)
                second[place] = jnp.where(low, one, three)
        return carry

    lax.fori_loop(0, blocks // GROUP, step, 0)


def apply_class(q, target, left_sector, right_sector, wavefunction, left_ops, right_ops):
    blocks, rows, cols = wavefunction.shape
    _, terms, sectors, _, _ = left_ops.shape
    per = rows // lax.axis_size("op")
    width = max(blocks, 128)
    outs = [
        pltpu.VMEM((blocks, count, cols), t) for _, count in PARTS[q] for t in (F32, BF16, BF16, BF16)
    ]
    flops = 2 * blocks * terms * (rows * rows * cols + rows * cols * cols)
    return pl.pallas_call(
        functools.partial(apply_kernel, q=q, per=per),
        out_shape=outs,
        in_specs=[pl.BlockSpec(memory_space=pltpu.HBM)] * 6,
        out_specs=[pl.BlockSpec(memory_space=pltpu.VMEM) for _ in outs],
        scratch_shapes=[
            pltpu.VMEM(wavefunction.shape, BF16),
            pltpu.VMEM((terms, sectors, rows, rows), BF16),
            pltpu.VMEM((terms, right_ops.shape[2], cols, cols), BF16),
            pltpu.VMEM((GROUP, rows, terms * cols), BF16),
            pltpu.SMEM((target.shape[0], width), jnp.int32),
            pltpu.SMEM(left_sector.shape, jnp.int32),
            pltpu.SMEM(right_sector.shape, jnp.int32),
            pltpu.SemaphoreType.DMA((3,)),
            pltpu.SemaphoreType.DMA((terms,)),
            pltpu.SemaphoreType.DMA((terms,)),
            pltpu.SemaphoreType.DMA((blocks // GROUP,)),
        ],
        compiler_params=pltpu.CompilerParams(vmem_limit_bytes=24 * MIB),
        cost_estimate=pl.CostEstimate(flops=flops, bytes_accessed=8 * MIB, transcendentals=0),
    )(*(pltpu.with_memory_space_constraint(a, pltpu.HBM) for a in (target, left_sector, right_sector, wavefunction, left_ops, right_ops)))


def shift(value, step, op_size):
    ring = [(i, (i + step) % op_size) for i in range(op_size)]
    return lax.ppermute(value, "op", ring)


def add(a, b):
    return (a.astype(F32) + b.astype(F32)).astype(BF16)


def place_kernel(source, *refs, layout, classes):
    arrived, out_hbm, out, out_sem = refs[:-3], *refs[-3:]
    blocks = out.shape[0]
    steps = out_sem.shape[0]
    chunk = blocks // steps

    def out_copy(c):
        part = pl.ds(c * chunk, chunk)
        return pltpu.make_async_copy(out.at[part], out_hbm.at[part], out_sem.at[c])

    def step(c, carry):
        for i in range(chunk):
            slot = c * chunk + i
            sources = [source[q, slot] for q in range(classes)]
            rows = {}
            for batch, row, (q, start, rows_here) in layout:
                for k in range(0, rows_here, 16):
                    term = arrived[batch][sources[q], row + k : row + k + 16].astype(F32)
                    rows.setdefault(start + k, []).append(term)
            for start, terms in rows.items():
                out[slot, start : start + 16] = functools.reduce(lambda a, b: a + b, terms)
        out_copy(c).start()
        return carry

    lax.fori_loop(0, steps, step, 0)
    for c in range(steps):
        out_copy(c).wait()


def per_device(wavefunction, left_ops, right_ops, left_sector, right_sector, target):
    shards = lax.axis_size("sec")
    op_size = lax.axis_size("op")
    own_sec = lax.axis_index("sec")
    blocks, rows, cols = wavefunction.shape
    classes = target.shape[0]
    per = rows // op_size
    operands = (target, left_sector, right_sector, wavefunction, left_ops, right_ops)
    parts = {}
    for q in range(classes):
        outs = apply_class(q, *operands)
        for k in range(len(PARTS[q])):
            parts[q, k] = outs[4 * k : 4 * k + 4]
    half = blocks // 2
    first = {key: (shift(up, 1, op_size), shift(down, -1, op_size)) for key, (_, up, down, _) in parts.items()}
    join = lambda values: values[0] if len(values) == 1 else jnp.concatenate(values, axis=1)
    summed = {}
    for group in JOINED:
        low = shift(join([add(parts[k][3][:half], first[k][0][:half]) for k in group]), 1, op_size)
        high = shift(join([add(parts[k][3][half:], first[k][1][half:]) for k in group]), -1, op_size)
        row = 0
        for key in group:
            rows_here = slice(row, row + PARTS[key[0]][key[1]][1])
            own, below, above = parts[key][0], *first[key]
            summed[key] = jnp.concatenate(
                [
                    own[:half] + above[:half].astype(F32) + low[:, rows_here].astype(F32),
                    own[half:] + below[half:].astype(F32) + high[:, rows_here].astype(F32),
                ],
                axis=0,
            ).astype(BF16)
            row = rows_here.stop
    arrived, layout = [], []
    for n, batch in enumerate(BATCHES):
        row = 0
        for q, k in batch:
            layout.append((n, row, (q, *PARTS[q][k])))
            row += PARTS[q][k][1]
        arrived.append(
            lax.all_to_all(join([summed[key] for key in batch]), "sec", split_axis=0, concat_axis=0, tiled=True)
        )
    by_source = target.reshape(classes, shards, blocks)
    slots = jnp.sum(jnp.where(by_source // blocks == own_sec, by_source % blocks, 0), axis=2)
    sources = jnp.sum(
        jnp.where(slots[:, None, :] == jnp.arange(blocks)[None, :, None], jnp.arange(shards, dtype=jnp.int32), 0), axis=2
    )
    sources = jnp.minimum(sources, shards - 1)
    steps = 4
    return pl.pallas_call(
        functools.partial(place_kernel, layout=layout, classes=classes),
        out_shape=jax.ShapeDtypeStruct((blocks, per, cols), F32),
        in_specs=[pl.BlockSpec(memory_space=pltpu.SMEM)] + [pl.BlockSpec(memory_space=pltpu.VMEM)] * len(arrived),
        out_specs=pl.BlockSpec(memory_space=pltpu.HBM),
        scratch_shapes=[pltpu.VMEM((blocks, per, cols), F32), pltpu.SemaphoreType.DMA((steps,))],
        compiler_params=pltpu.CompilerParams(vmem_limit_bytes=16 * MIB),
        name="place_blocks",
    )(sources, *arrived)


def solution(mesh):
    in_specs = (
        P("sec", None, None),
        P(None, "op", None, None, None),
        P(None, "op", None, None, None),
        P("sec"),
        P("sec"),
        P(),
    )

    return jax.shard_map(per_device, mesh=mesh, in_specs=in_specs, out_specs=P("sec", "op", None), check_vma=False)
```
